32 devices in a mesh: ctx: 8 (over z, x), tp: 4 (over y, core).
Axes of the slice: x: 2, y: 2, z: 4, core: 2. Of those that a mesh axis runs over, the one named last changes fastest.
Arguments:
- queries: bfloat16 [1024, 8192], P('ctx', 'tp'), may hold values from -6 to 6
- keys: bfloat16 [4096, 1024], P(('ctx', 'tp')), may hold values from -6 to 6
- values: bfloat16 [4096, 1024], P(('ctx', 'tp')), may hold values from -6 to 6
- grad_out: bfloat16 [1024, 8192], P('ctx', 'tp'), may hold values from -6 to 6
- readers: int32 [8, 4], replicated, may hold values from -1 to 15, as said below
- token_mask: int32 [1024, 4], P('ctx'), may hold values from 0 to 1
- image_len: int32 [16], replicated, may hold values from 64 to 256
Outputs:
- grad_queries: bfloat16 [1024, 8192], P('ctx', 'tp')
- grad_keys: float32 [4096, 1024], P(('ctx', 'tp'))
- grad_values: float32 [4096, 1024], P(('ctx', 'tp'))
The draws below stay inside these ranges and needn't reach their ends.
Inputs may be any that keep to these rules, and one draw needn't show every extreme that they name: `readers`: image m is owned by ctx index m // 2. Row c holds 2 runs of 2 consecutive slots; each run names 2 different images of one owner c - k, the first run with k = 0, the others with different k from 1 to 3; a run whose owner c - k is below 0 is all -1.
All inputs are finite; a program needn't handle non-finite values.
Results may differ from the reference program's by a relative error of at most 0.012.
Values may be sent and summed in bfloat16 or wider, within the bound.
A program may use at most 64 MiB of HBM per device.

```python
import jax
import jax.numpy as jnp
from jax import lax

HEADS = 64
KVH = 8
HD = 128
TOK_DEV = 128
IMG_DEV = 2
ITOK = 256
SLOTS = 4
CAP = 2
WIN = 4
TOKENS = 1024
IMAGES = 16
N_CTX = 8


def reader_table(key):
    base = jax.random.fold_in(key, 11)
    groups = SLOTS // CAP
    offset_keys = jax.random.split(jax.random.fold_in(base, 1), N_CTX)
    offsets = jax.vmap(lambda subkey: jax.random.permutation(subkey, WIN - 1) + 1)(offset_keys).astype(jnp.int32)
    group_offsets = jnp.concatenate([jnp.zeros((N_CTX, 1), jnp.int32), offsets[:, :groups - 1]], axis=1)
    pick_keys = jax.random.split(jax.random.fold_in(base, 2), N_CTX * groups)
    picks = jax.vmap(lambda subkey: jax.random.permutation(subkey, IMG_DEV)[:CAP])(pick_keys)
    picks = picks.astype(jnp.int32).reshape(N_CTX, groups, CAP)
    owners = jnp.arange(N_CTX, dtype=jnp.int32)[:, None] - group_offsets
    image_ids = owners[:, :, None] * IMG_DEV + picks
    image_ids = jnp.where(owners[:, :, None] >= 0, image_ids, -1)
    return image_ids.reshape(N_CTX, SLOTS).astype(jnp.int32)


def mask_table(key):
    return jax.random.randint(jax.random.fold_in(key, 13), (TOKENS, SLOTS), 0, 2, dtype=jnp.int32)


def key_table(key):
    base = jnp.clip(jax.random.normal(jax.random.fold_in(key, 17), (IMAGES * ITOK, KVH * HD), jnp.float32), -6.0, 6.0)
    return base


def draw_readers(key, part):
    return reader_table(key)


def draw_token_mask(key, part):
    return mask_table(key)


def draw_keys(key, part):
    return key_table(key).astype(jnp.bfloat16)


def draw_queries(key, part):
    base = jnp.clip(jax.random.normal(jax.random.fold_in(key, 19), (TOKENS, HEADS * HD), jnp.float32), -6.0, 6.0)
    return base.astype(jnp.bfloat16)


def plant(result, rng, low, top_value):
    extent = result.shape
    spot = [jax.random.randint(jax.random.fold_in(rng, axis), (), 0, extent[axis]) for axis in range(len(extent))]
    result = result.at[tuple(spot)].set(low)
    longest = extent.index(max(extent))
    spot[longest] = (spot[longest] + 1) % extent[longest]
    return result.at[tuple(spot)].set(top_value)


def levels(key, dims, cuts, least, high):
    def one(dim, parts):
        heights = jax.random.uniform(jax.random.fold_in(jax.random.fold_in(key, 6), dim), (parts,), jnp.float32, least / len(cuts), high / len(cuts))
        return jnp.repeat(jnp.exp(heights), dims[dim] // parts).reshape((-1,) + (1,) * (len(dims) - dim - 1))

    loudness = one(*cuts[0])
    for cut in cuts[1:]:
        loudness = loudness * one(*cut)
    return loudness


def noise(key, shape, deviation, most, cuts=(), kind=jnp.bfloat16):
    factor_of = levels(key, shape, cuts, -0.22, 0.18) if cuts else 1.0
    entries = jax.random.normal(key, shape, jnp.float32) * deviation * factor_of
    return jnp.minimum(jnp.maximum(entries, -most), most).astype(kind)


def setup_inputs(seed: int = 0) -> dict:
    key_list = jax.random.split(jax.random.key(seed), 8)
    queries = draw_queries(jax.random.fold_in(key_list[7], 71), 0)
    keys = draw_keys(jax.random.fold_in(key_list[7], 71), 0)
    values = noise(key_list[2], (IMAGES * ITOK, KVH * HD), 1.0, 6.0, ((0, 32),))
    grad_out = noise(key_list[3], (TOKENS, HEADS * HD), 1.0, 6.0, ((0, 8), (1, 4)))
    readers = draw_readers(jax.random.fold_in(key_list[7], 71), 0)
    token_mask = draw_token_mask(jax.random.fold_in(key_list[7], 71), 0)
    image_len = plant(jax.random.randint(key_list[6], (IMAGES,), ITOK // 4, ITOK + 1), jax.random.fold_in(key_list[6], 1), ITOK // 4, ITOK).astype(jnp.int32)
    return dict(queries=queries, keys=keys, values=values, grad_out=grad_out, readers=readers, token_mask=token_mask, image_len=image_len)


masked_score = -1e+30

def head_grad(query, upstream, key_head, value_head, allowed, scaling):
    scores = jnp.dot(query, key_head.T, preferred_element_type=jnp.float32) * scaling
    scores = jnp.where(allowed, scores, masked_score)
    row_max = lax.optimization_barrier(jnp.max(scores, axis=1, keepdims=True))
    exponent = jnp.where(allowed, jnp.exp(scores - row_max), 0.0)
    totals = jnp.maximum(lax.optimization_barrier(jnp.sum(exponent, axis=1, keepdims=True)), 1.0)
    weights = exponent / totals
    weights_half = weights.astype(jnp.bfloat16)
    attended = jnp.dot(weights_half, value_head, preferred_element_type=jnp.float32)
    row_dot = lax.optimization_barrier(jnp.sum(upstream.astype(jnp.float32) * attended, axis=1, keepdims=True))
    grad_value = jnp.dot(weights_half.T, upstream, preferred_element_type=jnp.float32)
    grad_weights = jnp.dot(upstream, value_head.T, preferred_element_type=jnp.float32)
    scores_half = (weights * (grad_weights - row_dot)).astype(jnp.bfloat16)
    grad_query = jnp.dot(scores_half, key_head, preferred_element_type=jnp.float32) * scaling
    grad_key = jnp.dot(scores_half.T, query, preferred_element_type=jnp.float32) * scaling
    return (grad_query, grad_key, grad_value)

def reference(queries, keys, values, grad_out, readers, token_mask, image_len):
    scaling = HD ** (-0.5)
    per_group = HEADS // KVH
    key_images = keys.reshape(IMAGES, ITOK, KVH, HD)
    value_images = values.reshape(IMAGES, ITOK, KVH, HD)
    positions = jnp.arange(ITOK, dtype=jnp.int32)

    def shard_step(carried, shard):
        grad_keys, grad_values = carried
        image_ids = readers[shard]
        present = image_ids >= 0
        safe_ids = jnp.maximum(image_ids, 0).astype(jnp.int32)
        lengths = image_len[safe_ids]
        start = (shard * TOK_DEV).astype(jnp.int32)
        query_rows = lax.dynamic_slice_in_dim(queries, start, TOK_DEV, 0).reshape(TOK_DEV, HEADS, HD)
        upstream_rows = lax.dynamic_slice_in_dim(grad_out, start, TOK_DEV, 0).reshape(TOK_DEV, HEADS, HD)
        mask_rows = lax.dynamic_slice_in_dim(token_mask, start, TOK_DEV, 0)
        allowed = (mask_rows[:, :, None] == 1) & present[None, :, None] & (positions[None, None, :] < lengths[None, :, None])
        allowed = allowed.reshape(TOK_DEV, SLOTS * ITOK)
        slot_keys = key_images[safe_ids].reshape(SLOTS * ITOK, KVH, HD)
        slot_values = value_images[safe_ids].reshape(SLOTS * ITOK, KVH, HD)
        query_parts = []
        key_parts = []
        value_parts = []
        for head_group in range(KVH):
            key_head = slot_keys[:, head_group]
            value_head = slot_values[:, head_group]

            def head_step(inner, pair):
                grad_query, grad_key, grad_value = head_grad(pair[0], pair[1], key_head, value_head, allowed, scaling)
                return ((inner[0] + grad_key, inner[1] + grad_value), grad_query)
            first = head_group * per_group
            pairs = (jnp.moveaxis(query_rows[:, first:first + per_group], 1, 0), jnp.moveaxis(upstream_rows[:, first:first + per_group], 1, 0))
            zeros = jnp.zeros((SLOTS * ITOK, HD), jnp.float32)
            (group_keys, group_values), group_queries = lax.scan(head_step, (zeros, zeros), pairs)
            query_parts.append(group_queries)
            key_parts.append(group_keys)
            value_parts.append(group_values)
        grad_query = jnp.moveaxis(jnp.concatenate(query_parts, axis=0), 0, 1).reshape(TOK_DEV, HEADS * HD)
        scale_mask = present.astype(jnp.float32)[:, None, None, None]
        slot_grad_keys = jnp.stack(key_parts, axis=1).reshape(SLOTS, ITOK, KVH, HD) * scale_mask
        slot_grad_values = jnp.stack(value_parts, axis=1).reshape(SLOTS, ITOK, KVH, HD) * scale_mask
        grad_keys = grad_keys.at[safe_ids].add(slot_grad_keys)
        grad_values = grad_values.at[safe_ids].add(slot_grad_values)
        return ((grad_keys, grad_values), grad_query.astype(jnp.bfloat16))
    zeros = jnp.zeros((IMAGES, ITOK, KVH, HD), jnp.float32)
    (grad_keys, grad_values), grad_queries = lax.scan(shard_step, (zeros, zeros), jnp.arange(N_CTX, dtype=jnp.int32))
    return (grad_queries.reshape(TOKENS, HEADS * HD), grad_keys.reshape(IMAGES * ITOK, KVH * HD), grad_values.reshape(IMAGES * ITOK, KVH * HD))
```

```python
import functools

import jax
import jax.numpy as jnp
from jax import lax
from jax.experimental import pallas as pl
from jax.experimental.pallas import tpu as pltpu
from jax.sharding import PartitionSpec as P

HD = 128
IMG_DEV = 2
SLOTS = 4
WIN = 4
MESH = pl.DeviceIdType.MESH
NEG = -1e30
LOG2E = 1.4426950408889634


def kernel(
    n_ctx, n_tp, groups, per_group,
    readers, image_len, q, go, k, v, tm,
    gq, gk, gv,
    *scratch,
):
    nch = 2 * groups
    kvb = scratch[:nch]
    (bias, kcat, vcat, qs, gs, wt, dst, acc, prem, s1, sc, se, rp, rd, rc, fin, fout,
     loc_sem, a_send, a_recv, f_send, f_recv, b_send, b_recv, z_send, z_recv) = scratch[nch:]
    rows = k.shape[0]
    half = rows * n_tp
    itok = half // IMG_DEV
    toks = q.shape[0]
    scaling = HD ** (-0.5)
    c = lax.axis_index("ctx")
    t = lax.axis_index("tp")
    even = lax.rem(c, 2) == 0
    odd = lax.rem(c, 2) == 1
    partner = c + 1 - 2 * lax.rem(c, 2)
    has_up = c + 2 < n_ctx
    has_down = c >= 2

    barrier = pltpu.get_barrier_semaphore()
    for d in range(1, n_tp):
        pl.semaphore_signal(barrier, inc=1, device_id=(c, lax.rem(t + d, n_tp)), device_id_type=MESH)
    pl.semaphore_signal(barrier, inc=1, device_id=(partner, t), device_id_type=MESH)

    @pl.when(has_up)
    def _():
        pl.semaphore_signal(barrier, inc=1, device_id=(c + 2, t), device_id_type=MESH)

    @pl.when(has_down)
    def _():
        pl.semaphore_signal(barrier, inc=1, device_id=(c - 2, t), device_id_type=MESH)

    both = has_up & has_down

    @pl.when(both)
    def _():
        pl.semaphore_wait(barrier, n_tp + 2)

    @pl.when(jnp.logical_not(both))
    def _():
        pl.semaphore_wait(barrier, n_tp + 1)

    def copy(src, dst_ref, send, recv, ctx, tp):
        return pltpu.make_async_remote_copy(
            src_ref=src, dst_ref=dst_ref, send_sem=send, recv_sem=recv,
            device_id=(ctx, tp), device_id_type=MESH,
        )

    def gather(ch, d):
        src = (k, v)[ch % 2]
        to = lax.rem(t + d, n_tp)
        cols = pl.ds(pl.multiple_of((to * groups + ch // 2) * HD, HD), HD)
        return copy(
            src.at[:, cols], kvb[ch].at[0, pl.ds(pl.multiple_of(t * rows, rows), rows)],
            a_send.at[d - 1, ch], a_recv.at[d - 1, ch], c, to,
        )

    def gather_own(ch):
        src = (k, v)[ch % 2]
        cols = pl.ds(pl.multiple_of((t * groups + ch // 2) * HD, HD), HD)
        return pltpu.make_async_copy(
            src.at[:, cols], kvb[ch].at[0, pl.ds(pl.multiple_of(t * rows, rows), rows)],
            loc_sem.at[ch],
        )

    for ch in range(nch):
        for d in range(1, n_tp):
            gather(ch, d).start()
        gather_own(ch).start()

    rem_id = readers[c, IMG_DEV]
    rem_ok = rem_id >= 0
    rem_owner = jnp.maximum(rem_id, 0) // IMG_DEV
    ksel = jnp.where(rem_ok, c - rem_owner, 0)
    kload = jnp.clip(ksel, 0, WIN - 1)
    up_row = jnp.minimum(c + 1, n_ctx - 1)
    up_id = readers[up_row, IMG_DEV]
    up_k = jnp.where(up_id >= 0, c + 1 - jnp.maximum(up_id, 0) // IMG_DEV, 0)
    for b in range(SLOTS):
        run = (b // IMG_DEV) * IMG_DEV
        owner = c if b < IMG_DEV else rem_owner
        image = owner * IMG_DEV + b % IMG_DEV
        length = image_len[image]
        if b >= IMG_DEV:
            length = jnp.where(rem_ok, length, 0)
        mask = jnp.where(readers[c, run] == image, tm[run : run + 1], tm[run + 1 : run + 2])
        live = jnp.where(mask == 1, length, 0)
        place = lax.broadcasted_iota(jnp.int32, (itok, toks), 0)
        block = jnp.where(place < live, 0.0, NEG).astype(jnp.float32)
        bias[pl.ds(b * itok, itok), :toks] = block
        bias[pl.ds(b * itok, itok), toks:] = block

    def own_next(ch):
        return copy(kvb[ch].at[0], kvb[ch].at[1], f_send.at[0, ch], f_recv.at[0, ch], partner, t)

    def own_up(ch):
        return copy(kvb[ch].at[0], kvb[ch].at[2], f_send.at[1, ch], f_recv.at[1, ch], c + 2, t)

    def two_back(ch):
        return copy(kvb[ch].at[2], kvb[ch].at[1], f_send.at[0, ch], f_recv.at[0, ch], partner, t)

    def one_up(ch):
        return copy(kvb[ch].at[1], kvb[ch].at[3], f_send.at[2, ch], f_recv.at[2, ch], c + 2, t)

    def two_next(ch):
        return copy(kvb[ch].at[2], kvb[ch].at[3], f_send.at[3, ch], f_recv.at[2, ch], partner, t)

    for ch in range(nch):
        for d in range(1, n_tp):
            gather(ch, d).wait_recv()
        gather_own(ch).wait()

        @pl.when(has_up)
        def _():
            own_up(ch).start()

        @pl.when(even)
        def _():
            own_next(ch).start()

    for ch in range(nch):
        @pl.when(has_down)
        def _():
            own_up(ch).wait_recv()

            @pl.when(even)
            def _():
                two_next(ch).start()

            @pl.when(odd)
            def _():
                two_back(ch).start()

        @pl.when(even & has_down)
        def _():
            two_back(ch).wait_recv()

            @pl.when(has_up)
            def _():
                one_up(ch).start()

        @pl.when(odd)
        def _():
            own_next(ch).wait_recv()

    def arrive(ch):
        @pl.when(odd & has_down)
        def _():
            two_next(ch).wait_recv()

        @pl.when(even & (c >= 4))
        def _():
            one_up(ch).wait_recv()

    def first_send(ch):
        @pl.when(odd)
        def _():
            copy(s1.at[ch], rp.at[ch], b_send.at[0, ch], b_recv.at[0, ch], partner, t).start()

        @pl.when(even & has_down)
        def _():
            copy(s1.at[ch], rd.at[ch], b_send.at[0, ch], b_recv.at[1, ch], c - 2, t).start()

    send_partial = jnp.where(odd, ((ksel == 1) | (ksel == 3)), ksel == 3)

    for g in range(groups):
        for ch in (2 * g, 2 * g + 1):
            arrive(ch)
        kcat[:half] = kvb[2 * g][0]
        kcat[half:] = kvb[2 * g][kload]
        vcat[:half] = kvb[2 * g + 1][0]
        vcat[half:] = kvb[2 * g + 1][kload]
        for h in range(per_group):
            cols = pl.ds((g * per_group + h) * HD, HD)
            qs[pl.ds(h * toks, toks)] = q[:, cols]
            gs[pl.ds(h * toks, toks)] = go[:, cols]
        kt = jnp.transpose(kcat[...])

        def pair_step(p, carry):
            span = pl.ds(pl.multiple_of(p * 2 * toks, 2 * toks), 2 * toks)
            nt = (((1,), (1,)), ((), ()))
            score = lax.dot_general(kcat[...], qs[span], nt, preferred_element_type=jnp.float32)
            x = score * (scaling * LOG2E) + bias[...]
            top = jnp.maximum(jnp.max(x, axis=0, keepdims=True), 0.1 * NEG)
            e = jnp.exp2(x - top)
            inv = 1.0 / jnp.maximum(jnp.sum(e, axis=0, keepdims=True), 1.0)
            w = e * inv
            wt[:, span] = w.astype(jnp.bfloat16)
            gw = lax.dot_general(vcat[...], gs[span], nt, preferred_element_type=jnp.float32)
            u = w * gw
            dot = jnp.sum(u, axis=0, keepdims=True)
            ds = (u - w * dot).astype(jnp.bfloat16)
            dst[:, span] = ds
            gqt = jnp.dot(kt, ds, preferred_element_type=jnp.float32) * scaling
            for i in range(2):
                cols = pl.ds(pl.multiple_of((g * per_group + 2 * p + i) * HD, HD), HD)
                gq[:, cols] = jnp.transpose(gqt[:, i * toks : (i + 1) * toks]).astype(jnp.bfloat16)
            return carry

        lax.fori_loop(0, per_group // 2, pair_step, 0)
        for ch, (lhs, rhs) in ((2 * g, (dst, qs)), (2 * g + 1, (wt, gs))):
            scale = scaling if ch % 2 == 0 else 1.0
            total = jnp.dot(lhs[...], rhs[...], preferred_element_type=jnp.float32) * scale
            acc[ch] = total[:half]
            part = jnp.where(rem_ok, total[half:], 0.0).astype(jnp.bfloat16)
            prem[ch] = part
            s1[ch] = jnp.where(send_partial, part, jnp.zeros_like(part))
            first_send(ch)

    def from_partner(ch):
        return copy(s1.at[ch], rp.at[ch], b_send.at[0, ch], b_recv.at[0, ch], partner, t)

    def three_down(ch):
        return copy(s1.at[ch], rd.at[ch], b_send.at[0, ch], b_recv.at[1, ch], c - 2, t)

    def two_down(ch):
        return copy(sc.at[ch], rc.at[ch], b_send.at[1, ch], b_recv.at[2, ch], c - 2, t)

    def one_next(ch):
        return copy(se.at[ch], rp.at[ch], b_send.at[2, ch], b_recv.at[0, ch], partner, t)

    def picked(ch, cond):
        part = prem[ch]
        return jnp.where(cond, part, jnp.zeros_like(part)).astype(jnp.float32)

    for ch in range(nch):
        @pl.when(even)
        def _():
            from_partner(ch).wait_recv()
            got = rp[ch].astype(jnp.float32)
            acc[ch] = acc[ch] + jnp.where(up_k == 1, got, 0.0)

            @pl.when(has_down)
            def _():
                sc[ch] = (picked(ch, ksel == 2) + jnp.where(up_k == 3, got, 0.0)).astype(jnp.bfloat16)
                two_down(ch).start()

        @pl.when(even & has_up)
        def _():
            three_down(ch).wait_recv()

        @pl.when(even & has_down & has_up)
        def _():
            se[ch] = (picked(ch, ksel == 1) + rd[ch].astype(jnp.float32)).astype(jnp.bfloat16)
            one_next(ch).start()

        @pl.when(even & has_down & (c + 2 >= n_ctx))
        def _():
            se[ch] = picked(ch, ksel == 1).astype(jnp.bfloat16)
            one_next(ch).start()

    def hand(ch, d):
        to = lax.rem(t + d, n_tp)
        return copy(
            fout.at[ch, pl.ds(pl.multiple_of(to * rows, rows), rows)], fin.at[d - 1, ch],
            z_send.at[d - 1, ch], z_recv.at[d - 1, ch], c, to,
        )

    for ch in range(nch):
        @pl.when(odd & has_down)
        def _():
            one_next(ch).wait_recv()
            sc[ch] = (picked(ch, ksel == 2) + rp[ch].astype(jnp.float32)).astype(jnp.bfloat16)
            two_down(ch).start()

    for ch in range(nch):
        @pl.when(has_up)
        def _():
            two_down(ch).wait_recv()
            acc[ch] = acc[ch] + rc[ch].astype(jnp.float32)

        fout[ch] = acc[ch].astype(jnp.bfloat16)
        for d in range(1, n_tp):
            hand(ch, d).start()

    def put(ch, who, block):
        out = (gk, gv)[ch % 2]
        out[:, pl.ds(pl.multiple_of((who * groups + ch // 2) * HD, HD), HD)] = block

    for ch in range(nch):
        put(ch, t, acc[ch, pl.ds(pl.multiple_of(t * rows, rows), rows)])
    for ch in range(nch):
        for d in range(1, n_tp):
            hand(ch, d).wait_recv()
            put(ch, lax.rem(t + n_tp - d, n_tp), fin[d - 1, ch].astype(jnp.float32))

    for ch in range(nch):
        for d in range(1, n_tp):
            gather(ch, d).wait_send()
            hand(ch, d).wait_send()

        @pl.when(has_up)
        def _():
            own_up(ch).wait_send()

        @pl.when(even)
        def _():
            own_next(ch).wait_send()

        @pl.when(odd)
        def _():
            from_partner(ch).wait_send()

        @pl.when(odd & has_down)
        def _():
            two_back(ch).wait_send()

        @pl.when(even & has_down)
        def _():
            two_next(ch).wait_send()
            three_down(ch).wait_send()
            one_next(ch).wait_send()

        @pl.when(even & has_down & has_up)
        def _():
            one_up(ch).wait_send()

        @pl.when(has_down)
        def _():
            two_down(ch).wait_send()


def on_device(n_ctx, n_tp, queries, keys, values, grad_out, readers, token_mask, image_len):
    rows, width = keys.shape
    groups = width // HD // n_tp
    toks = queries.shape[0]
    per_group = queries.shape[1] // HD // groups
    nch = 2 * groups
    half = rows * n_tp
    bf, f32 = jnp.bfloat16, jnp.float32
    vm = pl.BlockSpec(memory_space=pltpu.VMEM)
    sm = pl.BlockSpec(memory_space=pltpu.SMEM)
    dma = pltpu.SemaphoreType.DMA
    item = pltpu.VMEM((nch, half, HD), bf)
    return pl.pallas_call(
        functools.partial(kernel, n_ctx, n_tp, groups, per_group),
        out_shape=(
            jax.ShapeDtypeStruct(queries.shape, bf),
            jax.ShapeDtypeStruct(keys.shape, f32),
            jax.ShapeDtypeStruct(keys.shape, f32),
        ),
        in_specs=[sm, sm, vm, vm, vm, vm, vm],
        out_specs=(vm, vm, vm),
        scratch_shapes=[pltpu.VMEM((WIN, half, HD), bf)] * nch
        + [
            pltpu.VMEM((2 * half, 2 * toks), f32),
            pltpu.VMEM((2 * half, HD), bf),
            pltpu.VMEM((2 * half, HD), bf),
            pltpu.VMEM((per_group * toks, HD), bf),
            pltpu.VMEM((per_group * toks, HD), bf),
            pltpu.VMEM((2 * half, per_group * toks), bf),
            pltpu.VMEM((2 * half, per_group * toks), bf),
            pltpu.VMEM((nch, half, HD), f32),
            item, item, item, item, item, item, item,
            pltpu.VMEM((n_tp - 1, nch, rows, HD), bf),
            item,
            dma((nch,)),
            dma((n_tp - 1, nch)), dma((n_tp - 1, nch)),
            dma((4, nch)), dma((3, nch)),
            dma((3, nch)), dma((3, nch)),
            dma((n_tp - 1, nch)), dma((n_tp - 1, nch)),
        ],
        compiler_params=pltpu.CompilerParams(
            collective_id=0, has_side_effects=True, vmem_limit_bytes=50 * 1024 * 1024
        ),
    )(readers, image_len, queries, grad_out, keys, values, token_mask.T)


def solution(mesh):
    n_ctx, n_tp = mesh.shape["ctx"], mesh.shape["tp"]
    return jax.shard_map(
        functools.partial(on_device, n_ctx, n_tp),
        mesh=mesh,
        in_specs=(
            P("ctx", "tp"),
            P(("ctx", "tp"), None),
            P(("ctx", "tp"), None),
            P("ctx", "tp"),
            P(),
            P("ctx", None),
            P(),
        ),
        out_specs=(P("ctx", "tp"), P(("ctx", "tp"), None), P(("ctx", "tp"), None)),
        check_vma=False,
    )
```

```python
import functools

import jax
import jax.numpy as jnp
from jax import lax
from jax.experimental import pallas as pl
from jax.experimental.pallas import tpu as pltpu
from jax.sharding import PartitionSpec as P

HD = 128
IMG_DEV = 2
SLOTS = 4
WIN = 4
MESH = pl.DeviceIdType.MESH
NEG = -1e30
LOG2E = 1.4426950408889634


def kernel(
    n_ctx, n_tp, groups, per_group,
    readers, image_len, q, go, k, v, tm,
    gq, gk, gv,
    *scratch,
):
    nch = 2 * groups
    kvb = scratch[:nch]
    (bias, kcat, vcat, qs, gs, wt, dst, acc, prem, s1, sc, se, rp, rd, rc, fin, fout, st,
     q_sem, loc_sem, a_send, a_recv, f_send, f_recv, b_send, b_recv, z_send, z_recv) = scratch[nch:]
    rows = k.shape[0]
    half = rows * n_tp
    itok = half // IMG_DEV
    toks = q.shape[0]
    scaling = HD ** (-0.5)
    c = lax.axis_index("ctx")
    t = lax.axis_index("tp")
    even = lax.rem(c, 2) == 0
    odd = lax.rem(c, 2) == 1
    partner = c + 1 - 2 * lax.rem(c, 2)
    has_up = c + 2 < n_ctx
    has_down = c >= 2

    barrier = pltpu.get_barrier_semaphore()
    for d in range(1, n_tp):
        pl.semaphore_signal(barrier, inc=1, device_id=(c, lax.rem(t + d, n_tp)), device_id_type=MESH)
    pl.semaphore_signal(barrier, inc=1, device_id=(partner, t), device_id_type=MESH)

    @pl.when(has_up)
    def _():
        pl.semaphore_signal(barrier, inc=1, device_id=(c + 2, t), device_id_type=MESH)

    @pl.when(has_down)
    def _():
        pl.semaphore_signal(barrier, inc=1, device_id=(c - 2, t), device_id_type=MESH)

    both = has_up & has_down

    @pl.when(both)
    def _():
        pl.semaphore_wait(barrier, n_tp + 2)

    @pl.when(jnp.logical_not(both))
    def _():
        pl.semaphore_wait(barrier, n_tp + 1)

    def copy(src, dst_ref, send, recv, ctx, tp):
        return pltpu.make_async_remote_copy(
            src_ref=src, dst_ref=dst_ref, send_sem=send, recv_sem=recv,
            device_id=(ctx, tp), device_id_type=MESH,
        )

    def gather(ch, d):
        src = (k, v)[ch % 2]
        to = lax.rem(t + d, n_tp)
        cols = pl.ds(pl.multiple_of((to * groups + ch // 2) * HD, HD), HD)
        return copy(
            src.at[:, cols], kvb[ch].at[0, pl.ds(pl.multiple_of(t * rows, rows), rows)],
            a_send.at[d - 1, ch], a_recv.at[d - 1, ch], c, to,
        )

    def gather_own(ch):
        src = (k, v)[ch % 2]
        cols = pl.ds(pl.multiple_of((t * groups + ch // 2) * HD, HD), HD)
        return pltpu.make_async_copy(
            src.at[:, cols], kvb[ch].at[0, pl.ds(pl.multiple_of(t * rows, rows), rows)],
            loc_sem.at[ch],
        )

    for ch in range(nch):
        for d in range(1, n_tp):
            gather(ch, d).start()
        gather_own(ch).start()

    def head_copy(which, h):
        src, into = ((q, qs), (go, gs))[which]
        return pltpu.make_async_copy(
            src.at[:, pl.ds(h * HD, HD)], into.at[pl.ds(h * toks, toks)], q_sem.at[which, h]
        )

    for h in range(groups * per_group):
        head_copy(0, h).start()
        head_copy(1, h).start()

    rem_id = readers[IMG_DEV, c]
    rem_ok = rem_id >= 0
    rem_owner = jnp.maximum(rem_id, 0) // IMG_DEV
    ksel = jnp.where(rem_ok, c - rem_owner, 0)
    near = jnp.where(ksel == 2, 2, jnp.where(ksel == 0, 0, 1))
    slot_of = (jnp.where(even & (ksel == 3), 3, near), near)
    side_id = readers[IMG_DEV, partner]
    side_k = jnp.where(side_id >= 0, partner - jnp.maximum(side_id, 0) // IMG_DEV, 0)
    for b in range(SLOTS):
        run = (b // IMG_DEV) * IMG_DEV
        owner = c if b < IMG_DEV else rem_owner
        image = owner * IMG_DEV + b % IMG_DEV
        length = image_len[image]
        if b >= IMG_DEV:
            length = jnp.where(rem_ok, length, 0)
        mask = jnp.where(readers[run, c] == image, tm[run : run + 1], tm[run + 1 : run + 2])
        live = jnp.where(mask == 1, length, 0)
        place = lax.broadcasted_iota(jnp.int32, (itok, toks), 0)
        block = jnp.where(place < live, 0.0, NEG).astype(jnp.float32)
        bias[pl.ds(b * itok, itok), :toks] = block
        bias[pl.ds(b * itok, itok), toks:] = block

    def own_up(ch):
        return copy(kvb[ch].at[0], kvb[ch].at[2], f_send.at[0, ch], f_recv.at[0, ch], c + 2, t)

    def side(ch, src):
        return copy(src, kvb[ch].at[1], f_send.at[1, ch], f_recv.at[1, ch], partner, t)

    def relay(ch):
        src = kvb[ch].at[1 + ch % 2]
        return copy(src, kvb[ch].at[3], f_send.at[2, ch], f_recv.at[2, ch], c + 2, t)

    for ch in range(nch):
        for d in range(1, n_tp):
            gather(ch, d).wait_recv()
        gather_own(ch).wait()

        @pl.when(has_up)
        def _():
            own_up(ch).start()

    def spread(ch):
        @pl.when(has_down)
        def _():
            own_up(ch).wait_recv()

        @pl.when(even & has_down)
        def _():
            st[ch] = jnp.where(side_k == 3, kvb[ch][2], kvb[ch][0])
            side(ch, st.at[ch]).start()

        @pl.when(even & jnp.logical_not(has_down))
        def _():
            side(ch, kvb[ch].at[0]).start()

        if ch % 2 == 0:
            @pl.when(odd & has_down)
            def _():
                side(ch, kvb[ch].at[2]).start()

            @pl.when(even & has_down)
            def _():
                side(ch, kvb[ch].at[0]).wait_recv()

                @pl.when(has_up)
                def _():
                    relay(ch).start()
        else:
            @pl.when(odd & has_down & has_up)
            def _():
                relay(ch).start()

            @pl.when(odd & (c >= 5))
            def _():
                relay(ch).wait_recv()
                st[ch] = jnp.where(side_k == 3, kvb[ch][3], kvb[ch][2])
                side(ch, st.at[ch]).start()

            @pl.when(odd & has_down & (c < 5))
            def _():
                side(ch, kvb[ch].at[2]).start()

    def arrive(ch):
        @pl.when(odd)
        def _():
            side(ch, kvb[ch].at[0]).wait_recv()

        if ch % 2 == 0:
            @pl.when(even & (c >= 4))
            def _():
                relay(ch).wait_recv()
        else:
            @pl.when(even & has_down)
            def _():
                side(ch, kvb[ch].at[0]).wait_recv()

    def to_side(ch):
        return copy(s1.at[ch], rp.at[ch], b_send.at[0, ch], b_recv.at[0, ch], partner, t)

    def three_down(ch):
        return copy(s1.at[ch], rd.at[ch], b_send.at[0, ch], b_recv.at[1, ch], c - 2, t)

    def two_down(ch):
        return copy(sc.at[ch], rc.at[ch], b_send.at[1, ch], b_recv.at[2, ch], c - 2, t)

    def pass_side(ch):
        return copy(se.at[ch], rp.at[ch], b_send.at[2, ch], b_recv.at[0, ch], partner, t)

    def pass_down(ch):
        return copy(se.at[ch], rd.at[ch], b_send.at[2, ch], b_recv.at[1, ch], c - 2, t)

    near_k = (ksel == 1) | (ksel == 3)

    def first_send(ch):
        part = prem[ch]
        wanted = near_k if ch % 2 else jnp.where(odd, near_k, ksel == 3)
        s1[ch] = jnp.where(wanted, part, jnp.zeros_like(part))

        @pl.when(odd)
        def _():
            to_side(ch).start()

        @pl.when(even & has_down)
        def _():
            (to_side if ch % 2 else three_down)(ch).start()

    def picked(ch, cond):
        part = prem[ch]
        return jnp.where(cond, part, jnp.zeros_like(part)).astype(jnp.float32)

    def even_mid(ch):
        @pl.when(even)
        def _():
            to_side(ch).wait_recv()
            got = rp[ch].astype(jnp.float32)

            @pl.when(has_down)
            def _():
                sc[ch] = (picked(ch, ksel == 2) + jnp.where(side_k == 3, got, 0.0)).astype(jnp.bfloat16)
                two_down(ch).start()

            acc[ch] = acc[ch] + jnp.where(side_k == 1, got, 0.0)

        if ch % 2 == 0:
            @pl.when(even & has_up)
            def _():
                three_down(ch).wait_recv()

            @pl.when(even & has_down & has_up)
            def _():
                se[ch] = (picked(ch, ksel == 1) + rd[ch].astype(jnp.float32)).astype(jnp.bfloat16)
                pass_side(ch).start()

            @pl.when(even & has_down & jnp.logical_not(has_up))
            def _():
                se[ch] = picked(ch, ksel == 1).astype(jnp.bfloat16)
                pass_side(ch).start()

    def odd_first(ch):
        if ch % 2:
            @pl.when(odd & has_down)
            def _():
                to_side(ch).wait_recv()

            @pl.when(odd & (c >= 5))
            def _():
                got = rp[ch]
                se[ch] = jnp.where(side_k == 3, got, jnp.zeros_like(got))
                pass_down(ch).start()

    def odd_mid(ch):
        if ch % 2 == 0:
            @pl.when(odd & has_down)
            def _():
                pass_side(ch).wait_recv()
                sc[ch] = (picked(ch, ksel == 2) + rp[ch].astype(jnp.float32)).astype(jnp.bfloat16)
                two_down(ch).start()
        else:
            def near_sum():
                got = rp[ch].astype(jnp.float32)
                return picked(ch, ksel == 2) + jnp.where(side_k == 1, got, 0.0)

            @pl.when(odd & has_down & has_up)
            def _():
                pass_down(ch).wait_recv()
                sc[ch] = (near_sum() + rd[ch].astype(jnp.float32)).astype(jnp.bfloat16)
                two_down(ch).start()

            @pl.when(odd & has_down & jnp.logical_not(has_up))
            def _():
                sc[ch] = near_sum().astype(jnp.bfloat16)
                two_down(ch).start()

    spread(0)
    spread(1)
    for g in range(groups):
        for ch in (2 * g, 2 * g + 1):
            arrive(ch)
        for h in range(g * per_group, (g + 1) * per_group):
            head_copy(0, h).wait()
            head_copy(1, h).wait()
        kcat[:half] = kvb[2 * g][0]
        kcat[half:] = kvb[2 * g][slot_of[0]]
        vcat[:half] = kvb[2 * g + 1][0]
        vcat[half:] = kvb[2 * g + 1][slot_of[1]]
        kt = jnp.transpose(kcat[...])
        base = g * per_group * toks

        def pair_step(p, carry):
            span = pl.ds(pl.multiple_of(p * 2 * toks, 2 * toks), 2 * toks)
            heads = pl.ds(pl.multiple_of(base + p * 2 * toks, 2 * toks), 2 * toks)
            nt = (((1,), (1,)), ((), ()))
            score = lax.dot_general(kcat[...], qs[heads], nt, preferred_element_type=jnp.float32)
            x = score * (scaling * LOG2E) + bias[...]
            top = jnp.maximum(jnp.max(x, axis=0, keepdims=True), 0.1 * NEG)
            e = jnp.exp2(x - top)
            inv = 1.0 / jnp.maximum(jnp.sum(e, axis=0, keepdims=True), 1.0)
            w = e * inv
            wt[:, span] = w.astype(jnp.bfloat16)
            gw = lax.dot_general(vcat[...], gs[heads], nt, preferred_element_type=jnp.float32)
            u = w * gw
            dot = jnp.sum(u, axis=0, keepdims=True)
            ds = (u - w * dot).astype(jnp.bfloat16)
            dst[:, span] = ds
            gqt = jnp.dot(kt, ds, preferred_element_type=jnp.float32) * scaling
            for i in range(2):
                cols = pl.ds(pl.multiple_of((g * per_group + 2 * p + i) * HD, HD), HD)
                gq[:, cols] = jnp.transpose(gqt[:, i * toks : (i + 1) * toks]).astype(jnp.bfloat16)
            return carry

        pairs = per_group // 2
        lax.fori_loop(0, pairs // 2, pair_step, 0)
        if g + 1 < groups:
            spread(2 * g + 2)
        if g > 0:
            even_mid(2 * g - 1)
        lax.fori_loop(pairs // 2, pairs, pair_step, 0)
        if g + 1 < groups:
            spread(2 * g + 3)
        if g > 0:
            odd_first(2 * g - 1)
            even_mid(2 * g - 2)
        own_rows = pl.ds(base, per_group * toks)
        for ch, (lhs, rhs) in ((2 * g, (dst, qs)), (2 * g + 1, (wt, gs))):
            scale = scaling if ch % 2 == 0 else 1.0
            total = jnp.dot(lhs[...], rhs[own_rows], preferred_element_type=jnp.float32) * scale
            acc[ch] = total[:half]
            prem[ch] = jnp.where(rem_ok, total[half:], 0.0).astype(jnp.bfloat16)
            first_send(ch)

    for ch in range(nch):
        if ch < nch - 2:
            odd_mid(ch)
    for ch in range(nch - 2, nch):
        even_mid(ch)
        odd_first(ch)
    for ch in range(nch - 2, nch):
        odd_mid(ch)

    def hand(ch, d):
        to = lax.rem(t + d, n_tp)
        return copy(
            fout.at[ch, pl.ds(pl.multiple_of(to * rows, rows), rows)], fin.at[d - 1, ch],
            z_send.at[d - 1, ch], z_recv.at[d - 1, ch], c, to,
        )

    for ch in range(nch):
        @pl.when(has_up)
        def _():
            two_down(ch).wait_recv()
            acc[ch] = acc[ch] + rc[ch].astype(jnp.float32)

        fout[ch] = acc[ch].astype(jnp.bfloat16)
        for d in range(1, n_tp):
            hand(ch, d).start()

    def put(ch, who, block):
        out = (gk, gv)[ch % 2]
        out[:, pl.ds(pl.multiple_of((who * groups + ch // 2) * HD, HD), HD)] = block

    for ch in range(nch):
        put(ch, t, acc[ch, pl.ds(pl.multiple_of(t * rows, rows), rows)])
    for ch in range(nch):
        for d in range(1, n_tp):
            hand(ch, d).wait_recv()
            put(ch, lax.rem(t + n_tp - d, n_tp), fin[d - 1, ch].astype(jnp.float32))

    for ch in range(nch):
        for d in range(1, n_tp):
            gather(ch, d).wait_send()
            hand(ch, d).wait_send()

        @pl.when(has_up)
        def _():
            own_up(ch).wait_send()

        @pl.when(even | has_down)
        def _():
            side(ch, kvb[ch].at[0]).wait_send()

        @pl.when((odd if ch % 2 else even) & has_down & has_up)
        def _():
            relay(ch).wait_send()

        @pl.when(odd | has_down)
        def _():
            to_side(ch).wait_send()

        @pl.when(has_down)
        def _():
            two_down(ch).wait_send()

        if ch % 2 == 0:
            @pl.when(even & has_down)
            def _():
                pass_side(ch).wait_send()
        else:
            @pl.when(odd & (c >= 5))
            def _():
                pass_down(ch).wait_send()


def on_device(n_ctx, n_tp, queries, keys, values, grad_out, readers, token_mask, image_len):
    rows, width = keys.shape
    groups = width // HD // n_tp
    toks = queries.shape[0]
    per_group = queries.shape[1] // HD // groups
    nch = 2 * groups
    half = rows * n_tp
    bf, f32 = jnp.bfloat16, jnp.float32
    vm = pl.BlockSpec(memory_space=pltpu.VMEM)
    hbm = pl.BlockSpec(memory_space=pltpu.HBM)
    sm = pl.BlockSpec(memory_space=pltpu.SMEM)
    dma = pltpu.SemaphoreType.DMA
    item = pltpu.VMEM((nch, half, HD), bf)
    return pl.pallas_call(
        functools.partial(kernel, n_ctx, n_tp, groups, per_group),
        out_shape=(
            jax.ShapeDtypeStruct(queries.shape, bf),
            jax.ShapeDtypeStruct(keys.shape, f32),
            jax.ShapeDtypeStruct(keys.shape, f32),
        ),
        in_specs=[sm, sm, hbm, hbm, hbm, hbm, vm],
        out_specs=(vm, vm, vm),
        scratch_shapes=[pltpu.VMEM((WIN, half, HD), bf)] * nch
        + [
            pltpu.VMEM((2 * half, 2 * toks), f32),
            pltpu.VMEM((2 * half, HD), bf),
            pltpu.VMEM((2 * half, HD), bf),
            pltpu.VMEM((groups * per_group * toks, HD), bf),
            pltpu.VMEM((groups * per_group * toks, HD), bf),
            pltpu.VMEM((2 * half, per_group * toks), bf),
            pltpu.VMEM((2 * half, per_group * toks), bf),
            pltpu.VMEM((nch, half, HD), f32),
            item, item, item, item, item, item, item,
            pltpu.VMEM((n_tp - 1, nch, rows, HD), bf),
            item, item,
            dma((2, groups * per_group)),
            dma((nch,)),
            dma((n_tp - 1, nch)), dma((n_tp - 1, nch)),
            dma((3, nch)), dma((3, nch)),
            dma((3, nch)), dma((3, nch)),
            dma((n_tp - 1, nch)), dma((n_tp - 1, nch)),
        ],
        compiler_params=pltpu.CompilerParams(
            collective_id=0, has_side_effects=True, vmem_limit_bytes=66_900_000
        ),
    )(readers.T, image_len, queries, grad_out, keys, values, token_mask.T)


def solution(mesh):
    n_ctx, n_tp = mesh.shape["ctx"], mesh.shape["tp"]
    return jax.shard_map(
        functools.partial(on_device, n_ctx, n_tp),
        mesh=mesh,
        in_specs=(
            P("ctx", "tp"),
            P(("ctx", "tp"), None),
            P(("ctx", "tp"), None),
            P("ctx", "tp"),
            P(),
            P("ctx", None),
            P(),
        ),
        out_specs=(P("ctx", "tp"), P(("ctx", "tp"), None), P(("ctx", "tp"), None)),
        check_vma=False,
    )
```

```python
import functools

import jax
import jax.numpy as jnp
from jax import lax
from jax.experimental import pallas as pl
from jax.experimental.pallas import tpu as pltpu
from jax.sharding import PartitionSpec as P

HD = 128
IMG_DEV = 2
SLOTS = 4
WIN = 4
MESH = pl.DeviceIdType.MESH
NEG = -1e30
LOG2E = 1.4426950408889634


def kernel(
    n_ctx, n_tp, groups, per_group,
    readers, image_len, q, go, k, v, tm,
    gq, gk, gv,
    *scratch,
):
    nch = 2 * groups
    kvb = scratch[:nch]
    (bias, kcat, vcat, qs, gs, wt, dst, acc, prem, s1, sc, se, rp, rd, rc, fin, fout,
     loc_sem, a_send, a_recv, f_send, f_recv, b_send, b_recv, z_send, z_recv) = scratch[nch:]
    rows = k.shape[0]
    half = rows * n_tp
    itok = half // IMG_DEV
    toks = q.shape[0]
    scaling = HD ** (-0.5)
    c = lax.axis_index("ctx")
    t = lax.axis_index("tp")
    even = lax.rem(c, 2) == 0
    odd = lax.rem(c, 2) == 1
    partner = c + 1 - 2 * lax.rem(c, 2)
    has_up = c + 2 < n_ctx
    has_down = c >= 2

    barrier = pltpu.get_barrier_semaphore()
    for d in range(1, n_tp):
        pl.semaphore_signal(barrier, inc=1, device_id=(c, lax.rem(t + d, n_tp)), device_id_type=MESH)
    pl.semaphore_signal(barrier, inc=1, device_id=(partner, t), device_id_type=MESH)

    @pl.when(has_up)
    def _():
        pl.semaphore_signal(barrier, inc=1, device_id=(c + 2, t), device_id_type=MESH)

    @pl.when(has_down)
    def _():
        pl.semaphore_signal(barrier, inc=1, device_id=(c - 2, t), device_id_type=MESH)

    both = has_up & has_down

    @pl.when(both)
    def _():
        pl.semaphore_wait(barrier, n_tp + 2)

    @pl.when(jnp.logical_not(both))
    def _():
        pl.semaphore_wait(barrier, n_tp + 1)

    def copy(src, dst_ref, send, recv, ctx, tp):
        return pltpu.make_async_remote_copy(
            src_ref=src, dst_ref=dst_ref, send_sem=send, recv_sem=recv,
            device_id=(ctx, tp), device_id_type=MESH,
        )

    def gather(ch, d):
        src = (k, v)[ch % 2]
        to = lax.rem(t + d, n_tp)
        cols = pl.ds(pl.multiple_of((to * groups + ch // 2) * HD, HD), HD)
        return copy(
            src.at[:, cols], kvb[ch].at[0, pl.ds(pl.multiple_of(t * rows, rows), rows)],
            a_send.at[d - 1, ch], a_recv.at[d - 1, ch], c, to,
        )

    def gather_own(ch):
        src = (k, v)[ch % 2]
        cols = pl.ds(pl.multiple_of((t * groups + ch // 2) * HD, HD), HD)
        return pltpu.make_async_copy(
            src.at[:, cols], kvb[ch].at[0, pl.ds(pl.multiple_of(t * rows, rows), rows)],
            loc_sem.at[ch],
        )

    for ch in range(nch):
        for d in range(1, n_tp):
            gather(ch, d).start()
        gather_own(ch).start()

    rem_id = readers[IMG_DEV, c]
    rem_ok = rem_id >= 0
    rem_owner = jnp.maximum(rem_id, 0) // IMG_DEV
    ksel = jnp.where(rem_ok, c - rem_owner, 0)
    kload = jnp.clip(ksel, 0, WIN - 1)
    up_row = jnp.minimum(c + 1, n_ctx - 1)
    up_id = readers[IMG_DEV, up_row]
    up_k = jnp.where(up_id >= 0, c + 1 - jnp.maximum(up_id, 0) // IMG_DEV, 0)
    for b in range(SLOTS):
        run = (b // IMG_DEV) * IMG_DEV
        owner = c if b < IMG_DEV else rem_owner
        image = owner * IMG_DEV + b % IMG_DEV
        length = image_len[image]
        if b >= IMG_DEV:
            length = jnp.where(rem_ok, length, 0)
        mask = jnp.where(readers[run, c] == image, tm[run : run + 1], tm[run + 1 : run + 2])
        live = jnp.where(mask == 1, length, 0)
        place = lax.broadcasted_iota(jnp.int32, (itok, toks), 0)
        block = jnp.where(place < live, 0.0, NEG).astype(jnp.float32)
        bias[pl.ds(b * itok, itok), :toks] = block
        bias[pl.ds(b * itok, itok), toks:] = block

    def own_next(ch):
        return copy(kvb[ch].at[0], kvb[ch].at[1], f_send.at[0, ch], f_recv.at[0, ch], partner, t)

    def own_up(ch):
        return copy(kvb[ch].at[0], kvb[ch].at[2], f_send.at[1, ch], f_recv.at[1, ch], c + 2, t)

    def two_back(ch):
        return copy(kvb[ch].at[2], kvb[ch].at[1], f_send.at[0, ch], f_recv.at[0, ch], partner, t)

    def one_up(ch):
        return copy(kvb[ch].at[1], kvb[ch].at[3], f_send.at[2, ch], f_recv.at[2, ch], c + 2, t)

    def two_next(ch):
        return copy(kvb[ch].at[2], kvb[ch].at[3], f_send.at[3, ch], f_recv.at[2, ch], partner, t)

    for ch in range(nch):
        for d in range(1, n_tp):
            gather(ch, d).wait_recv()
        gather_own(ch).wait()

        @pl.when(has_up)
        def _():
            own_up(ch).start()

        @pl.when(even)
        def _():
            own_next(ch).start()

    def near(ch):
        @pl.when(has_down)
        def _():
            own_up(ch).wait_recv()

            @pl.when(even)
            def _():
                two_next(ch).start()

            @pl.when(odd)
            def _():
                two_back(ch).start()

    def far(ch):
        @pl.when(even & has_down)
        def _():
            two_back(ch).wait_recv()

            @pl.when(has_up)
            def _():
                one_up(ch).start()

        @pl.when(odd)
        def _():
            own_next(ch).wait_recv()

    near(0)
    for ch in range(1, nch):
        near(ch)
        far(ch - 1)
    far(nch - 1)

    def arrive(ch):
        @pl.when(odd & has_down)
        def _():
            two_next(ch).wait_recv()

        @pl.when(even & (c >= 4))
        def _():
            one_up(ch).wait_recv()

    def first_send(ch):
        @pl.when(odd)
        def _():
            copy(s1.at[ch], rp.at[ch], b_send.at[0, ch], b_recv.at[0, ch], partner, t).start()

        @pl.when(even & has_down)
        def _():
            copy(s1.at[ch], rd.at[ch], b_send.at[0, ch], b_recv.at[1, ch], c - 2, t).start()

    send_partial = jnp.where(odd, ((ksel == 1) | (ksel == 3)), ksel == 3)

    for g in range(groups):
        for ch in (2 * g, 2 * g + 1):
            arrive(ch)
        kcat[:half] = kvb[2 * g][0]
        kcat[half:] = kvb[2 * g][kload]
        vcat[:half] = kvb[2 * g + 1][0]
        vcat[half:] = kvb[2 * g + 1][kload]
        for h in range(per_group):
            cols = pl.ds((g * per_group + h) * HD, HD)
            qs[pl.ds(h * toks, toks)] = q[:, cols]
            gs[pl.ds(h * toks, toks)] = go[:, cols]
        kt = jnp.transpose(kcat[...])

        def pair_step(p, carry):
            span = pl.ds(pl.multiple_of(p * 2 * toks, 2 * toks), 2 * toks)
            nt = (((1,), (1,)), ((), ()))
            score = lax.dot_general(kcat[...], qs[span], nt, preferred_element_type=jnp.float32)
            x = score * (scaling * LOG2E) + bias[...]
            top = jnp.maximum(jnp.max(x, axis=0, keepdims=True), 0.1 * NEG)
            e = jnp.exp2(x - top)
            inv = 1.0 / jnp.maximum(jnp.sum(e, axis=0, keepdims=True), 1.0)
            w = e * inv
            wt[:, span] = w.astype(jnp.bfloat16)
            gw = lax.dot_general(vcat[...], gs[span], nt, preferred_element_type=jnp.float32)
            u = w * gw
            dot = jnp.sum(u, axis=0, keepdims=True)
            ds = (u - w * dot).astype(jnp.bfloat16)
            dst[:, span] = ds
            gqt = jnp.dot(kt, ds, preferred_element_type=jnp.float32) * scaling
            for i in range(2):
                cols = pl.ds(pl.multiple_of((g * per_group + 2 * p + i) * HD, HD), HD)
                gq[:, cols] = jnp.transpose(gqt[:, i * toks : (i + 1) * toks]).astype(jnp.bfloat16)
            return carry

        lax.fori_loop(0, per_group // 2, pair_step, 0)
        for ch, (lhs, rhs) in ((2 * g, (dst, qs)), (2 * g + 1, (wt, gs))):
            scale = scaling if ch % 2 == 0 else 1.0
            total = jnp.dot(lhs[...], rhs[...], preferred_element_type=jnp.float32) * scale
            acc[ch] = total[:half]
            part = jnp.where(rem_ok, total[half:], 0.0).astype(jnp.bfloat16)
            prem[ch] = part
            s1[ch] = jnp.where(send_partial, part, jnp.zeros_like(part))
            first_send(ch)

    def from_partner(ch):
        return copy(s1.at[ch], rp.at[ch], b_send.at[0, ch], b_recv.at[0, ch], partner, t)

    def three_down(ch):
        return copy(s1.at[ch], rd.at[ch], b_send.at[0, ch], b_recv.at[1, ch], c - 2, t)

    def two_down(ch):
        return copy(sc.at[ch], rc.at[ch], b_send.at[1, ch], b_recv.at[2, ch], c - 2, t)

    def one_next(ch):
        return copy(se.at[ch], rp.at[ch], b_send.at[2, ch], b_recv.at[0, ch], partner, t)

    def picked(ch, cond):
        part = prem[ch]
        return jnp.where(cond, part, jnp.zeros_like(part)).astype(jnp.float32)

    for ch in range(nch):
        @pl.when(even)
        def _():
            from_partner(ch).wait_recv()
            got = rp[ch].astype(jnp.float32)
            acc[ch] = acc[ch] + jnp.where(up_k == 1, got, 0.0)

            @pl.when(has_down)
            def _():
                sc[ch] = (picked(ch, ksel == 2) + jnp.where(up_k == 3, got, 0.0)).astype(jnp.bfloat16)
                two_down(ch).start()

        @pl.when(even & has_up)
        def _():
            three_down(ch).wait_recv()

        @pl.when(even & has_down & has_up)
        def _():
            se[ch] = (picked(ch, ksel == 1) + rd[ch].astype(jnp.float32)).astype(jnp.bfloat16)
            one_next(ch).start()

        @pl.when(even & has_down & (c + 2 >= n_ctx))
        def _():
            se[ch] = picked(ch, ksel == 1).astype(jnp.bfloat16)
            one_next(ch).start()

    def hand(ch, d):
        to = lax.rem(t + d, n_tp)
        return copy(
            fout.at[ch, pl.ds(pl.multiple_of(to * rows, rows), rows)], fin.at[d - 1, ch],
            z_send.at[d - 1, ch], z_recv.at[d - 1, ch], c, to,
        )

    for ch in range(nch):
        @pl.when(odd & has_down)
        def _():
            one_next(ch).wait_recv()
            sc[ch] = (picked(ch, ksel == 2) + rp[ch].astype(jnp.float32)).astype(jnp.bfloat16)
            two_down(ch).start()

    for ch in range(nch):
        @pl.when(has_up)
        def _():
            two_down(ch).wait_recv()
            acc[ch] = acc[ch] + rc[ch].astype(jnp.float32)

        fout[ch] = acc[ch].astype(jnp.bfloat16)
        for d in range(1, n_tp):
            hand(ch, d).start()

    def put(ch, who, block):
        out = (gk, gv)[ch % 2]
        out[:, pl.ds(pl.multiple_of((who * groups + ch // 2) * HD, HD), HD)] = block

    for ch in range(nch):
        put(ch, t, acc[ch, pl.ds(pl.multiple_of(t * rows, rows), rows)])
    for ch in range(nch):
        for d in range(1, n_tp):
            hand(ch, d).wait_recv()
            put(ch, lax.rem(t + n_tp - d, n_tp), fin[d - 1, ch].astype(jnp.float32))

    for ch in range(nch):
        for d in range(1, n_tp):
            gather(ch, d).wait_send()
            hand(ch, d).wait_send()

        @pl.when(has_up)
        def _():
            own_up(ch).wait_send()

        @pl.when(even)
        def _():
            own_next(ch).wait_send()

        @pl.when(odd)
        def _():
            from_partner(ch).wait_send()

        @pl.when(odd & has_down)
        def _():
            two_back(ch).wait_send()

        @pl.when(even & has_down)
        def _():
            two_next(ch).wait_send()
            three_down(ch).wait_send()
            one_next(ch).wait_send()

        @pl.when(even & has_down & has_up)
        def _():
            one_up(ch).wait_send()

        @pl.when(has_down)
        def _():
            two_down(ch).wait_send()


def on_device(n_ctx, n_tp, queries, keys, values, grad_out, readers, token_mask, image_len):
    rows, width = keys.shape
    groups = width // HD // n_tp
    toks = queries.shape[0]
    per_group = queries.shape[1] // HD // groups
    nch = 2 * groups
    half = rows * n_tp
    bf, f32 = jnp.bfloat16, jnp.float32
    vm = pl.BlockSpec(memory_space=pltpu.VMEM)
    sm = pl.BlockSpec(memory_space=pltpu.SMEM)
    dma = pltpu.SemaphoreType.DMA
    item = pltpu.VMEM((nch, half, HD), bf)
    return pl.pallas_call(
        functools.partial(kernel, n_ctx, n_tp, groups, per_group),
        out_shape=(
            jax.ShapeDtypeStruct(queries.shape, bf),
            jax.ShapeDtypeStruct(keys.shape, f32),
            jax.ShapeDtypeStruct(keys.shape, f32),
        ),
        in_specs=[sm, sm, vm, vm, vm, vm, vm],
        out_specs=(vm, vm, vm),
        scratch_shapes=[pltpu.VMEM((WIN, half, HD), bf)] * nch
        + [
            pltpu.VMEM((2 * half, 2 * toks), f32),
            pltpu.VMEM((2 * half, HD), bf),
            pltpu.VMEM((2 * half, HD), bf),
            pltpu.VMEM((per_group * toks, HD), bf),
            pltpu.VMEM((per_group * toks, HD), bf),
            pltpu.VMEM((2 * half, per_group * toks), bf),
            pltpu.VMEM((2 * half, per_group * toks), bf),
            pltpu.VMEM((nch, half, HD), f32),
            item, item, item, item, item, item, item,
            pltpu.VMEM((n_tp - 1, nch, rows, HD), bf),
            item,
            dma((nch,)),
            dma((n_tp - 1, nch)), dma((n_tp - 1, nch)),
            dma((4, nch)), dma((3, nch)),
            dma((3, nch)), dma((3, nch)),
            dma((n_tp - 1, nch)), dma((n_tp - 1, nch)),
        ],
        compiler_params=pltpu.CompilerParams(
            collective_id=0, has_side_effects=True, vmem_limit_bytes=50 * 1024 * 1024
        ),
    )(readers.T, image_len, queries, grad_out, keys, values, token_mask.T)


def solution(mesh):
    n_ctx, n_tp = mesh.shape["ctx"], mesh.shape["tp"]
    return jax.shard_map(
        functools.partial(on_device, n_ctx, n_tp),
        mesh=mesh,
        in_specs=(
            P("ctx", "tp"),
            P(("ctx", "tp"), None),
            P(("ctx", "tp"), None),
            P("ctx", "tp"),
            P(),
            P("ctx", None),
            P(),
        ),
        out_specs=(P("ctx", "tp"), P(("ctx", "tp"), None), P(("ctx", "tp"), None)),
        check_vma=False,
    )
```
